32 devices in a mesh: sub: 8 (over y, x, core), col: 4 (over z).
Axes of the slice: x: 2, y: 2, z: 4, core: 2. Of those that a mesh axis runs over, the one named last changes fastest.
Arguments:
- state_init: float32 [128, 8192], P('col', 'sub'), may hold values from -3 to 3
- load_cols: float32 [128, 8192], P('col', 'sub'), may hold values from -6 to 6
- stiff_diag: bfloat16 [1024, 8192], P(None, 'sub'), may hold values from -0.1875 to 0.1875
- stiff_rim: bfloat16 [1024, 8192], P(None, 'sub'), may hold values from -0.1875 to 0.1875
- inverse: bfloat16 [2048, 8192], P(None, 'sub'), may hold values from -0.125 to 0.125
- ov_rows: int32 [8, 1024], P('sub'), may hold values from 0 to 1023, as said below
- ov_count: int32 [8], P('sub'), may hold values from 512 to 1024, as said below
- coarse_basis: bfloat16 [8192, 192], P('sub'), may hold values from -0.1875 to 0.1875
- coarse_map: bfloat16 [1536, 1536], P('sub', 'col'), may hold values from -0.21875 to 0.21875
Outputs:
- solution: float32 [128, 8192], P('col', 'sub')
- residual: float32 [128, 8192], P('col', 'sub')
The draws below stay inside these ranges and needn't reach their ends.
Inputs may be any that keep to these rules, and one draw needn't show every extreme that they name: `ov_rows`: each row holds 1024 different rim positions. `ov_count`: some subdomain uses all 1024 margin slots in every draw.
All inputs are finite; a program needn't handle non-finite values.
Results may differ from the reference program's by a relative error of at most 0.0075.
Values may be sent and summed in bfloat16 or wider, within the bound.
A program may use at most 64 MiB of HBM per device.

```python
import jax
import jax.numpy as jnp
from jax import lax

R = 1024
H = 512
OV = 1024
SMAX = 2048
NC = 192
ITERS = 2
N_ROWS = 8192
K = 128
NCOARSE = 1536
N_SUB = 8
N_COL = 4


def draw_ov_rows(key, part):
    keys = jax.random.split(jax.random.fold_in(key, 11), N_SUB)
    return jax.vmap(lambda single: jax.random.permutation(single, 2 * H)[:OV])(keys).astype(jnp.int32)


def draw_ov_count(key, part):
    first_key, second_key = jax.random.split(jax.random.fold_in(key, 23))
    counts = jax.random.randint(first_key, (N_SUB,), OV // 2, OV + 1)
    fullest = jax.random.randint(second_key, (), 0, N_SUB)
    return jnp.where(jnp.arange(N_SUB) == fullest, OV, counts).astype(jnp.int32)


def strengthened(array, stream_key, source, target, blocks, factor):
    owner, partner = [(jnp.arange(array.shape[axis_at]) // (array.shape[axis_at] // blocks)).reshape([-1 if axis == axis_at else 1 for axis in range(array.ndim)]) for axis_at in (source, target)]
    chosen = jax.random.permutation(stream_key, blocks)[partner]
    strong = (owner == chosen) | (owner == (partner + blocks // 2) % blocks)
    return jnp.where(strong, factor * array, array)


def shard_levels(rng, dims, shards, smallest, largest):
    factor_of = 1.0
    for dim, blocks in shards:
        steps = jax.random.uniform(jax.random.fold_in(jax.random.fold_in(rng, 6), dim), (blocks,), jnp.float32, smallest / len(shards), largest / len(shards))
        factor_of = factor_of * jnp.repeat(jnp.exp(steps), dims[dim] // blocks).reshape((-1,) + (1,) * (len(dims) - 1 - dim))
    return factor_of


def centred(own_key, extent, width, limit, cuts=(), kind=jnp.bfloat16):
    loudness = shard_levels(own_key, extent, cuts, -0.22, 0.18) if cuts else 1.0
    values = jax.random.normal(own_key, extent, jnp.float32) * width * loudness
    return jnp.minimum(jnp.maximum(values, -limit), limit).astype(kind)


def gaussian_with(key, extent, spread, limit, cuts, heavy, kind=jnp.bfloat16):
    values = spread * jax.random.normal(key, extent, jnp.float32)
    if cuts:
        values = values * shard_levels(key, extent, cuts, -0.22, 0.18)
    return jnp.clip(strengthened(values, jax.random.fold_in(key, 3), *heavy), -limit, limit).astype(kind)


def setup_inputs(seed: int = 0) -> dict:
    key_list = jax.random.split(jax.random.key(seed), 10)
    return {
        "state_init": centred(key_list[0], (K, N_ROWS), 0.5, 3.0, ((0, 4), (1, 8)), jnp.float32),
        "load_cols": centred(key_list[1], (K, N_ROWS), 1.0, 6.0, ((0, 4), (1, 8)), jnp.float32),
        "stiff_diag": centred(key_list[2], (R, N_ROWS), R ** -0.5, 0.1875, ((1, 8),)),
        "stiff_rim": centred(key_list[3], (2 * H, N_ROWS), (2 * H) ** -0.5, 0.1875, ((1, 8),)),
        "inverse": centred(key_list[4], (SMAX, N_ROWS), SMAX ** -0.5, 0.125, ((1, 8),)),
        "ov_rows": draw_ov_rows(jax.random.fold_in(key_list[9], 71), 0),
        "ov_count": draw_ov_count(jax.random.fold_in(key_list[9], 71), 0),
        "coarse_basis": centred(key_list[7], (N_ROWS, NC), R ** -0.5, 0.1875, ((0, 8),)),
        "coarse_map": gaussian_with(key_list[8], (NCOARSE, NCOARSE), NCOARSE ** -0.5, 0.21875, ((0, 8), (1, 4)), (0, 1, 8, 2.0)),
    }


cubic_coef = 0.1


def to_bf16(values):
    return lax.optimization_barrier(values.astype(jnp.bfloat16)).astype(jnp.float32)


def neighbour_rims(blocks):
    edge = jnp.zeros_like(blocks[:, :1, :H])
    before = jnp.concatenate([edge, blocks[:, :-1, R - H:]], axis=1)
    after = jnp.concatenate([blocks[:, 1:, :H], edge], axis=1)
    return jnp.concatenate([before, after], axis=2)


def residual_of(current, load_cols, diag_blocks, rim_blocks):
    columns = current.shape[0]
    rounded = to_bf16(current).reshape(columns, N_SUB, R)
    border = neighbour_rims(rounded)
    applied = jnp.einsum('ksi,isj->ksj', rounded, diag_blocks) + jnp.einsum('ksi,isj->ksj', border, rim_blocks)
    return load_cols - applied.reshape(columns, N_SUB * R) - cubic_coef * current * current * current


def reference(state_init, load_cols, stiff_diag, stiff_rim, inverse, ov_rows, ov_count, coarse_basis, coarse_map):
    diag_blocks = stiff_diag.astype(jnp.float32).reshape(R, N_SUB, R)
    rim_blocks = stiff_rim.astype(jnp.float32).reshape(2 * H, N_SUB, R)
    solve_blocks = inverse.astype(jnp.float32).reshape(SMAX, N_SUB, R)
    basis_blocks = coarse_basis.astype(jnp.float32).reshape(N_SUB, R, NC)
    live = jnp.arange(OV, dtype=jnp.int32)[None, :] < ov_count[:, None]
    current = state_init
    columns = current.shape[0]
    for iteration in range(ITERS):
        residual_now = residual_of(current, load_cols, diag_blocks, rim_blocks)
        rounded = to_bf16(residual_now).reshape(columns, N_SUB, R)
        border = neighbour_rims(rounded)
        positions = jnp.broadcast_to(ov_rows[None], (columns, N_SUB, OV)).astype(jnp.int32)
        picked = jnp.take_along_axis(border, positions, axis=2)
        picked = jnp.where(live[None], picked, jnp.zeros_like(picked))
        local_rhs = jnp.concatenate([rounded, picked], axis=2)
        fine_part = jnp.einsum('ksi,isj->ksj', local_rhs, solve_blocks)
        coefficients = jnp.einsum('ksi,sic->ksc', rounded, basis_blocks)
        coefficients = coefficients.reshape(columns, N_SUB * NC).astype(jnp.bfloat16)
        coarse = jnp.dot(coefficients, coarse_map, preferred_element_type=jnp.float32)
        coarse = to_bf16(coarse).reshape(columns, N_COL, N_SUB, NC // N_COL)
        coarse = jnp.transpose(coarse, (0, 2, 1, 3)).reshape(columns, N_SUB, NC)
        coarse_lift = jnp.einsum('ksc,sic->ksi', coarse, basis_blocks)
        current = current + (fine_part + coarse_lift).reshape(columns, N_SUB * R)
    final_residual = residual_of(current, load_cols, diag_blocks, rim_blocks)
    return current, final_residual
```

```python
import functools

import jax
import jax.numpy as jnp
from jax import lax
from jax.experimental import pallas as pl
from jax.experimental.pallas import tpu as pltpu
from jax.sharding import PartitionSpec as P

ITERS = 2

cubic_coef = 0.1
MESH = pl.DeviceIdType.MESH
F32 = jnp.float32
BF16 = jnp.bfloat16


def dot(a, b):
    return jnp.dot(a, b, preferred_element_type=F32)


def dot_nt(a, b):
    return lax.dot_general(a, b, (((1,), (1,)), ((), ())), preferred_element_type=F32)


def kernel(
    n, m,
    state_hbm, load_hbm, diag_hbm, rim_hbm, inv_hbm, ov_hbm, count_ref, basis_hbm, map_hbm,
    solution_ref, residual_ref,
    cur, load, diag, rim, inv, ov, basis, maps, invp, turned, zmap,
    sent, halo, part_out, part_in,
    local_sem, halo_send, halo_recv, map_send, map_recv, part_send, part_recv,
):
    me_s = lax.axis_index("sub")
    me_c = lax.axis_index("col")
    rows, width = cur.shape
    h = halo.shape[3]
    nc = basis.shape[1]
    per = nc // m
    slots = ov.shape[1]
    half = inv.shape[0] - slots

    def fetch(index, source, target):
        copy = pltpu.make_async_copy(source, target, local_sem.at[index])
        copy.start()
        return copy

    get_state = fetch(0, state_hbm, cur)
    get_map = fetch(1, map_hbm, maps.at[me_c])
    get_diag = fetch(2, diag_hbm, diag)
    get_rim = fetch(3, rim_hbm, rim)
    get_load = fetch(4, load_hbm, load)
    get_basis = fetch(5, basis_hbm, basis)
    get_ov = fetch(6, ov_hbm, ov)
    get_inv = fetch(7, inv_hbm, inv)

    barrier = pltpu.get_barrier_semaphore()
    for k in range(1, n):
        pl.semaphore_signal(barrier, inc=1, device_id={"sub": lax.rem(me_s + k, n)}, device_id_type=MESH)
    for k in range(1, m):
        pl.semaphore_signal(barrier, inc=1, device_id={"col": lax.rem(me_c + k, m)}, device_id_type=MESH)

    for e in range(2 * ITERS + 1):
        @pl.when(me_s == 0)
        def _():
            halo[e, 0] = jnp.zeros((rows, h), BF16)

        @pl.when(me_s == n - 1)
        def _():
            halo[e, 1] = jnp.zeros((rows, h), BF16)

    get_state.wait()
    sent[0] = cur[...].astype(BF16)
    get_map.wait()
    pl.semaphore_wait(barrier, n + m - 2)

    def to_next(e):
        return pltpu.make_async_remote_copy(
            src_ref=sent.at[e, :, pl.ds(width - h, h)], dst_ref=halo.at[e, 0],
            send_sem=halo_send.at[e, 0], recv_sem=halo_recv.at[e, 0],
            device_id={"sub": lax.rem(me_s + 1, n)}, device_id_type=MESH)

    def to_prev(e):
        return pltpu.make_async_remote_copy(
            src_ref=sent.at[e, :, pl.ds(0, h)], dst_ref=halo.at[e, 1],
            send_sem=halo_send.at[e, 1], recv_sem=halo_recv.at[e, 1],
            device_id={"sub": lax.rem(me_s + n - 1, n)}, device_id_type=MESH)

    def halo_start(e):
        @pl.when(me_s < n - 1)
        def _():
            to_next(e).start()

        @pl.when(me_s > 0)
        def _():
            to_prev(e).start()

    def halo_wait(e):
        @pl.when(me_s > 0)
        def _():
            to_next(e).wait_recv()

        @pl.when(me_s < n - 1)
        def _():
            to_prev(e).wait_recv()

    def halo_done(e):
        @pl.when(me_s < n - 1)
        def _():
            to_next(e).wait_send()

        @pl.when(me_s > 0)
        def _():
            to_prev(e).wait_send()

    def map_copy(peer, slot):
        return pltpu.make_async_remote_copy(
            src_ref=maps.at[slot], dst_ref=maps.at[slot],
            send_sem=map_send.at[peer], recv_sem=map_recv.at[slot],
            device_id={"col": peer}, device_id_type=MESH)

    def part_copy(it, peer, slot):
        return pltpu.make_async_remote_copy(
            src_ref=part_out.at[it, peer], dst_ref=part_in.at[it, slot],
            send_sem=part_send.at[it, peer], recv_sem=part_recv.at[it, slot],
            device_id={"sub": peer}, device_id_type=MESH)

    halo_start(0)
    for k in range(1, m):
        map_copy(lax.rem(me_c + k, m), me_c).start()

    def residual(e, first):
        if first:
            get_diag.wait()
        acc = dot(sent[e], diag[...])
        if first:
            get_rim.wait()
            get_load.wait()
        halo_wait(e)
        acc = acc + dot(halo[e, 0], rim[:h]) + dot(halo[e, 1], rim[h:])
        v = cur[...]
        return load[...] - acc - cubic_coef * v * v * v

    def turn_map():
        across = n * per
        eye = (
            lax.broadcasted_iota(jnp.int32, (across, across), 0)
            == lax.broadcasted_iota(jnp.int32, (across, across), 1)
        ).astype(F32).astype(BF16)
        for a in range(m):
            turned[a] = dot_nt(eye, maps[a])
        for s in range(n):
            zmap[s] = jnp.concatenate(
                [turned[a, s * per : (s + 1) * per, :] for a in range(m)], axis=0
            ).astype(BF16)

    def partials(it, coefficients):
        for s in range(n):
            part_out[it, s] = dot_nt(coefficients, zmap[s]).astype(BF16)
        for k in range(1, n):
            part_copy(it, lax.rem(me_s + k, n), me_s).start()
        part_in[it, me_s] = part_out[it, me_s]

    def permuted_inverse():
        used = ov[...]
        slot = lax.broadcasted_iota(jnp.int32, used.shape, 1)
        used = jnp.where(slot < count_ref[0], used, -1)
        chunk = 256

        def step(i, carry):
            at = i * chunk
            place = lax.broadcasted_iota(jnp.int32, (chunk, slots), 0) + at
            pick = (place == used).astype(F32).astype(BF16)
            invp[pl.ds(pl.multiple_of(at, chunk), chunk), :] = dot(pick, inv[half:, :]).astype(BF16)
            return carry

        lax.fori_loop(0, 2 * h // chunk, step, 0)

    for it in range(ITERS):
        first = it == 0
        rb = residual(2 * it, first).astype(BF16)
        e = 2 * it + 1
        sent[e] = rb
        halo_start(e)
        if first:
            get_basis.wait()
        coefficients = dot(rb, basis[...]).astype(BF16)
        if not first:
            partials(it, coefficients)
        if first:
            get_inv.wait()
            get_ov.wait()
            permuted_inverse()
        fine = dot(rb, inv[:half, :])
        halo_wait(e)
        fine = fine + dot(halo[e, 0], invp[:h, :]) + dot(halo[e, 1], invp[h:, :])
        if first:
            for k in range(1, m):
                map_copy(me_c, lax.rem(me_c + k, m)).wait_recv()
            turn_map()
            partials(it, coefficients)
        for k in range(1, n):
            part_copy(it, me_s, lax.rem(me_s + k, n)).wait_recv()
        total = part_in[it, 0].astype(F32)
        for s in range(1, n):
            total = total + part_in[it, s].astype(F32)
        lift = dot_nt(total.astype(BF16), basis[...])
        v = cur[...] + (fine + lift)
        cur[...] = v
        sent[e + 1] = v.astype(BF16)
        halo_start(e + 1)

    solution_ref[...] = cur[...]
    residual_ref[...] = residual(2 * ITERS, False)

    for e in range(2 * ITERS + 1):
        halo_done(e)
    for k in range(1, m):
        map_copy(lax.rem(me_c + k, m), me_c).wait_send()
    for it in range(ITERS):
        for k in range(1, n):
            part_copy(it, lax.rem(me_s + k, n), me_s).wait_send()


def body(n, m, state_init, load_cols, stiff_diag, stiff_rim, inverse, ov_rows, ov_count, coarse_basis, coarse_map):
    rows, width = state_init.shape
    h = stiff_rim.shape[0] // 2
    nc = coarse_basis.shape[1]
    trades = 2 * ITERS + 1
    hbm = pl.BlockSpec(memory_space=pl.ANY)
    vmem = pl.BlockSpec(memory_space=pltpu.VMEM)
    smem = pl.BlockSpec(memory_space=pltpu.SMEM)
    dma = pltpu.SemaphoreType.DMA
    out = jax.ShapeDtypeStruct((rows, width), F32)
    return pl.pallas_call(
        functools.partial(kernel, n, m),
        out_shape=(out, out),
        in_specs=[hbm, hbm, hbm, hbm, hbm, hbm, smem, hbm, hbm],
        out_specs=(vmem, vmem),
        scratch_shapes=[
            pltpu.VMEM((rows, width), F32),
            pltpu.VMEM((rows, width), F32),
            pltpu.VMEM(stiff_diag.shape, BF16),
            pltpu.VMEM(stiff_rim.shape, BF16),
            pltpu.VMEM(inverse.shape, BF16),
            pltpu.VMEM(ov_rows.shape, jnp.int32),
            pltpu.VMEM(coarse_basis.shape, BF16),
            pltpu.VMEM((m,) + coarse_map.shape, BF16),
            pltpu.VMEM((2 * h, width), BF16),
            pltpu.VMEM((m, coarse_map.shape[1], nc), F32),
            pltpu.VMEM((n, nc, nc), BF16),
            pltpu.VMEM((trades, rows, width), BF16),
            pltpu.VMEM((trades, 2, rows, h), BF16),
            pltpu.VMEM((ITERS, n, rows, nc), BF16),
            pltpu.VMEM((ITERS, n, rows, nc), BF16),
            dma((8,)),
            dma((trades, 2)),
            dma((trades, 2)),
            dma((m,)),
            dma((m,)),
            dma((ITERS, n)),
            dma((ITERS, n)),
        ],
        compiler_params=pltpu.CompilerParams(collective_id=0, has_side_effects=True),
        name="schwarz",
    )(state_init, load_cols, stiff_diag, stiff_rim, inverse, ov_rows, ov_count, coarse_basis, coarse_map)


def solution(mesh):
    in_specs = (
        P("col", "sub"),
        P("col", "sub"),
        P(None, "sub"),
        P(None, "sub"),
        P(None, "sub"),
        P("sub", None),
        P("sub"),
        P("sub", None),
        P("sub", "col"),
    )
    out_specs = (P("col", "sub"), P("col", "sub"))
    step = functools.partial(body, mesh.shape["sub"], mesh.shape["col"])
    return jax.shard_map(step, mesh=mesh, in_specs=in_specs, out_specs=out_specs, check_vma=False)
```

```python
import functools

import jax
import jax.numpy as jnp
from jax import lax
from jax.experimental import pallas as pl
from jax.experimental.pallas import tpu as pltpu
from jax.sharding import PartitionSpec as P

ITERS = 2
PIECES = 4

cubic_coef = 0.1
MESH = pl.DeviceIdType.MESH
F32 = jnp.float32
BF16 = jnp.bfloat16


def dot(a, b):
    return jnp.dot(a, b, preferred_element_type=F32)


def diagonal(size):
    place = [lax.broadcasted_iota(jnp.int32, (size, size), axis) for axis in (0, 1)]
    return (place[0] == place[1]).astype(F32).astype(BF16)


def dot_nt(a, b):
    return lax.dot_general(a, b, (((1,), (1,)), ((), ())), preferred_element_type=F32)


def kernel(
    n, m,
    state_hbm, load_hbm, diag_hbm, rim_hbm, inv_hbm, ov_hbm, count_hbm, basis_hbm, map_hbm,
    before_ref, change_ref, applied_ref,
    cur, load, diag, rim, inv, ov, count, basis, upright, maps, invp, turned, zmap,
    sent, halo, part_out, part_in,
    local_sem, halo_send, halo_recv, map_send, map_recv, relay_send, part_send, part_recv,
):
    me_s = lax.axis_index("sub")
    me_c = lax.axis_index("col")
    rows, width = cur.shape
    h = halo.shape[3]
    nc = basis.shape[0]
    per = nc // m
    slots = ov.shape[1]
    half = inv.shape[0] - slots

    barrier = pltpu.get_barrier_semaphore()
    for k in range(1, n):
        pl.semaphore_signal(barrier, inc=1, device_id={"sub": lax.rem(me_s + k, n)}, device_id_type=MESH)
    for k in range(1, m):
        pl.semaphore_signal(barrier, inc=1, device_id={"col": lax.rem(me_c + k, m)}, device_id_type=MESH)

    def fetch(index, source, target):
        copy = pltpu.make_async_copy(source, target, local_sem.at[index])
        copy.start()
        return copy

    get_state = fetch(0, state_hbm, cur)
    get_map = fetch(1, map_hbm, maps.at[me_c])
    get_diag = fetch(2, diag_hbm, diag)
    get_rim = fetch(3, rim_hbm, rim)
    get_load = fetch(4, load_hbm, load)
    get_basis = fetch(5, basis_hbm, basis)
    get_ov = fetch(6, ov_hbm, ov)
    get_count = fetch(7, count_hbm, count)
    get_inv = fetch(8, inv_hbm, inv)

    for e in range(2 * ITERS + 1):
        @pl.when(me_s == 0)
        def _():
            halo[e, 0] = jnp.zeros((rows, h), BF16)

        @pl.when(me_s == n - 1)
        def _():
            halo[e, 1] = jnp.zeros((rows, h), BF16)

    get_state.wait()
    sent[0] = cur[...].astype(BF16)
    get_map.wait()
    pl.semaphore_wait(barrier, n + m - 2)

    def to_next(e):
        return pltpu.make_async_remote_copy(
            src_ref=sent.at[e, :, pl.ds(width - h, h)], dst_ref=halo.at[e, 0],
            send_sem=halo_send.at[e, 0], recv_sem=halo_recv.at[e, 0],
            device_id={"sub": lax.rem(me_s + 1, n)}, device_id_type=MESH)

    def to_prev(e):
        return pltpu.make_async_remote_copy(
            src_ref=sent.at[e, :, pl.ds(0, h)], dst_ref=halo.at[e, 1],
            send_sem=halo_send.at[e, 1], recv_sem=halo_recv.at[e, 1],
            device_id={"sub": lax.rem(me_s + n - 1, n)}, device_id_type=MESH)

    def halo_start(e):
        @pl.when(me_s < n - 1)
        def _():
            to_next(e).start()

        @pl.when(me_s > 0)
        def _():
            to_prev(e).start()

    def halo_wait(e):
        @pl.when(me_s > 0)
        def _():
            to_next(e).wait_recv()

        @pl.when(me_s < n - 1)
        def _():
            to_prev(e).wait_recv()

    def halo_done(e):
        @pl.when(me_s < n - 1)
        def _():
            to_next(e).wait_send()

        @pl.when(me_s > 0)
        def _():
            to_prev(e).wait_send()

    relayed = m >= 4 and nc % (16 * PIECES) == 0
    pieces = PIECES if relayed else 1
    tall = nc // pieces
    upper = (2 * me_c) // m

    def map_copy(peer, slot, piece):
        return pltpu.make_async_remote_copy(
            src_ref=maps.at[slot, pl.ds(piece * tall, tall), :],
            dst_ref=maps.at[slot, pl.ds(piece * tall, tall), :],
            send_sem=map_send.at[peer, piece], recv_sem=map_recv.at[slot, piece],
            device_id={"col": peer}, device_id_type=MESH)

    def relay_copy(peer, slot, piece):
        return pltpu.make_async_remote_copy(
            src_ref=maps.at[slot, pl.ds(piece * tall, tall), :],
            dst_ref=maps.at[slot, pl.ds(piece * tall, tall), :],
            send_sem=relay_send.at[piece], recv_sem=map_recv.at[slot, piece],
            device_id={"col": peer}, device_id_type=MESH)

    def own_maps(act):
        for gap in range(m - 1 - relayed, 0, -1):
            for piece in range(pieces):
                @pl.when(me_c >= gap)
                def _():
                    act(map_copy(me_c - gap, me_c, piece))

                @pl.when(me_c + gap < m)
                def _():
                    act(map_copy(me_c + gap, me_c, piece))

    def relay(piece):
        if relayed:
            @pl.when(me_c == 1)
            def _():
                map_copy(1, m - 1, piece).wait_recv()
                relay_copy(0, m - 1, piece).start()

            @pl.when(me_c == m - 2)
            def _():
                map_copy(m - 2, 0, piece).wait_recv()
                relay_copy(m - 1, 0, piece).start()

    def relay_done():
        if relayed:
            for piece in range(pieces):
                @pl.when(me_c == 1)
                def _():
                    relay_copy(0, m - 1, piece).wait_send()

                @pl.when(me_c == m - 2)
                def _():
                    relay_copy(m - 1, 0, piece).wait_send()

    def part_copy(it, peer, slot):
        return pltpu.make_async_remote_copy(
            src_ref=part_out.at[it, peer], dst_ref=part_in.at[it, slot],
            send_sem=part_send.at[it, peer], recv_sem=part_recv.at[it, slot],
            device_id={"sub": peer}, device_id_type=MESH)

    halo_start(0)
    own_maps(lambda copy: copy.start())
    get_diag.wait()

    def stand_basis():
        block = 256
        for at in range(0, width, block):
            upright[at : at + block, :] = dot_nt(diagonal(block), basis[:, at : at + block]).astype(BF16)

    def applied(e, first):
        acc = dot(sent[e], diag[...])
        if first:
            get_basis.wait()
            stand_basis()
            get_rim.wait()
        halo_wait(e)
        return acc + dot(halo[e, 0], rim[:h]) + dot(halo[e, 1], rim[h:])

    def residual(e, first):
        acc = applied(e, first)
        if first:
            get_load.wait()
        v = cur[...]
        return load[...] - acc - cubic_coef * v * v * v

    def turn(j):
        flipped = dot_nt(diagonal(n * per), maps[j])
        if per % 16 == 0:
            for s in range(n):
                zmap[s, pl.ds(pl.multiple_of(j * per, 16), per), :] = flipped[s * per : (s + 1) * per].astype(BF16)
        else:
            turned[j] = flipped

    def turn_maps():
        for i in range(m):
            j = upper * (m - 1 - i) + (1 - upper) * i
            early = (me_c == 1) & (j == m - 1) | (me_c == m - 2) & (j == 0) if relayed else me_c < 0

            @pl.when((j != me_c) & jnp.logical_not(early))
            def _():
                for piece in range(pieces):
                    map_copy(me_c, j, piece).wait_recv()

            turn(j)
        if per % 16:
            for s in range(n):
                zmap[s] = jnp.concatenate(
                    [turned[a, s * per : (s + 1) * per, :] for a in range(m)], axis=0
                ).astype(BF16)

    def partials(it, coefficients):
        for s in range(n):
            part_out[it, s] = dot_nt(coefficients, zmap[s]).astype(BF16)
        for k in range(1, n):
            part_copy(it, lax.rem(me_s + k, n), me_s).start()
        part_in[it, me_s] = part_out[it, me_s]

    def permuted_inverse():
        used = ov[...]
        slot = lax.broadcasted_iota(jnp.int32, used.shape, 1)
        used = jnp.where(slot < count[0], used, -1)
        chunk = 2 * h // 4
        for i in range(4):
            place = lax.broadcasted_iota(jnp.int32, (chunk, slots), 0) + i * chunk
            pick = (place == used).astype(F32).astype(BF16)
            invp[i * chunk : (i + 1) * chunk, :] = dot(pick, inv[half:, :]).astype(BF16)
            if i == 1 and pieces > 1:
                relay(1)

    for it in range(ITERS):
        first = it == 0
        rb = residual(2 * it, first).astype(BF16)
        e = 2 * it + 1
        sent[e] = rb
        halo_start(e)
        coefficients = dot(rb, upright[...]).astype(BF16)
        if not first:
            partials(it, coefficients)
        if first:
            relay(0)
            get_inv.wait()
            get_ov.wait()
            get_count.wait()
            permuted_inverse()
        fine = dot(rb, inv[:half, :])
        halo_wait(e)
        fine = fine + dot(halo[e, 0], invp[:h, :]) + dot(halo[e, 1], invp[h:, :])
        if first:
            for piece in range(2, pieces):
                relay(piece)
            turn_maps()
            partials(it, coefficients)
        for k in range(1, n):
            part_copy(it, me_s, lax.rem(me_s + k, n)).wait_recv()
        total = part_in[it, 0].astype(F32)
        for s in range(1, n):
            total = total + part_in[it, s].astype(F32)
        lift = dot(total.astype(BF16), basis[...])
        change = fine + lift
        v = cur[...] + change
        if it == ITERS - 1:
            before_ref[...] = cur[...]
            change_ref[...] = change
        else:
            cur[...] = v
        sent[e + 1] = v.astype(BF16)
        halo_start(e + 1)

    applied_ref[...] = applied(2 * ITERS, False)

    for e in range(2 * ITERS + 1):
        halo_done(e)
    own_maps(lambda copy: copy.wait_send())
    relay_done()
    for it in range(ITERS):
        for k in range(1, n):
            part_copy(it, lax.rem(me_s + k, n), me_s).wait_send()


def body(n, m, state_init, load_cols, stiff_diag, stiff_rim, inverse, ov_rows, ov_count, coarse_basis, coarse_map):
    rows, width = state_init.shape
    h = stiff_rim.shape[0] // 2
    basis_t = coarse_basis.T
    nc = basis_t.shape[0]
    trades = 2 * ITERS + 1
    hbm = pl.BlockSpec(memory_space=pl.ANY)
    vmem = pl.BlockSpec(memory_space=pltpu.VMEM)
    dma = pltpu.SemaphoreType.DMA
    out = jax.ShapeDtypeStruct((rows, width), F32)
    before, change, product = pl.pallas_call(
        functools.partial(kernel, n, m),
        out_shape=(out, out, out),
        in_specs=[hbm] * 9,
        out_specs=(vmem, vmem, vmem),
        scratch_shapes=[
            pltpu.VMEM((rows, width), F32),
            pltpu.VMEM((rows, width), F32),
            pltpu.VMEM(stiff_diag.shape, BF16),
            pltpu.VMEM(stiff_rim.shape, BF16),
            pltpu.VMEM(inverse.shape, BF16),
            pltpu.VMEM(ov_rows.shape, jnp.int32),
            pltpu.SMEM((1,), jnp.int32),
            pltpu.VMEM(basis_t.shape, BF16),
            pltpu.VMEM(coarse_basis.shape, BF16),
            pltpu.VMEM((m,) + coarse_map.shape, BF16),
            pltpu.VMEM((2 * h, width), BF16),
            pltpu.VMEM((m, coarse_map.shape[1], nc), F32),
            pltpu.VMEM((n, nc, nc), BF16),
            pltpu.VMEM((trades, rows, width), BF16),
            pltpu.VMEM((trades, 2, rows, h), BF16),
            pltpu.VMEM((ITERS, n, rows, nc), BF16),
            pltpu.VMEM((ITERS, n, rows, nc), BF16),
            dma((9,)),
            dma((trades, 2)),
            dma((trades, 2)),
            dma((m, PIECES)),
            dma((m, PIECES)),
            dma((PIECES,)),
            dma((ITERS, n)),
            dma((ITERS, n)),
        ],
        compiler_params=pltpu.CompilerParams(collective_id=0, has_side_effects=True),
        name="schwarz",
    )(state_init, load_cols, stiff_diag, stiff_rim, inverse, ov_rows, ov_count, basis_t, coarse_map)
    current = before + change
    return current, load_cols - product - cubic_coef * current * current * current


def solution(mesh):
    in_specs = (
        P("col", "sub"),
        P("col", "sub"),
        P(None, "sub"),
        P(None, "sub"),
        P(None, "sub"),
        P("sub", None),
        P("sub"),
        P("sub", None),
        P("sub", "col"),
    )
    out_specs = (P("col", "sub"), P("col", "sub"))
    step = functools.partial(body, mesh.shape["sub"], mesh.shape["col"])
    return jax.shard_map(step, mesh=mesh, in_specs=in_specs, out_specs=out_specs, check_vma=False)
```

```python
import functools

import jax
import jax.numpy as jnp
from jax import lax
from jax.experimental import pallas as pl
from jax.experimental.pallas import tpu as pltpu
from jax.sharding import PartitionSpec as P

ITERS = 2
PIECES = 4

cubic_coef = 0.1
MESH = pl.DeviceIdType.MESH
F32 = jnp.float32
BF16 = jnp.bfloat16


def packed_shape(rows, nc):
    return (rows * nc // 128, 128) if nc % 128 == 64 and rows % 32 == 0 else (rows, nc)


def pack(block):
    rows, nc = block.shape
    if packed_shape(rows, nc) == block.shape:
        return block
    full = nc - nc % 128
    tail = jnp.concatenate([block[: rows // 2, full:], block[rows // 2 :, full:]], axis=1)
    return jnp.concatenate([block[:, at : at + 128] for at in range(0, full, 128)] + [tail], axis=0)


def unpack(block, rows, nc):
    if packed_shape(rows, nc) == (rows, nc):
        return block
    count = nc // 128
    tail = block[rows * count :]
    tail = jnp.concatenate([tail[:, :64], tail[:, 64:]], axis=0)
    return jnp.concatenate([block[rows * i : rows * (i + 1)] for i in range(count)] + [tail], axis=1)


def dot(a, b):
    return jnp.dot(a, b, preferred_element_type=F32)


def diagonal(size):
    place = [lax.broadcasted_iota(jnp.int32, (size, size), axis) for axis in (0, 1)]
    return (place[0] == place[1]).astype(F32).astype(BF16)


def dot_nt(a, b):
    return lax.dot_general(a, b, (((1,), (1,)), ((), ())), preferred_element_type=F32)


def kernel(
    n, m,
    state_hbm, load_hbm, diag_hbm, rim_hbm, inv_hbm, ov_hbm, count_hbm, basis_hbm, map_hbm,
    before_ref, change_ref, applied_ref,
    cur, load, diag, rim, inv, ov, count, basis, upright, maps, invp, turned, zmap,
    sent, halo, part_out, part_in,
    local_sem, halo_send, halo_recv, map_send, map_recv, relay_send, part_send, part_recv,
):
    me_s = lax.axis_index("sub")
    me_c = lax.axis_index("col")
    rows, width = cur.shape
    h = halo.shape[3]
    nc = basis.shape[0]
    per = nc // m
    slots = ov.shape[1]
    half = inv.shape[0] - slots

    barrier = pltpu.get_barrier_semaphore()
    for k in range(1, n):
        pl.semaphore_signal(barrier, inc=1, device_id={"sub": lax.rem(me_s + k, n)}, device_id_type=MESH)
    for k in range(1, m):
        pl.semaphore_signal(barrier, inc=1, device_id={"col": lax.rem(me_c + k, m)}, device_id_type=MESH)

    def fetch(index, source, target):
        copy = pltpu.make_async_copy(source, target, local_sem.at[index])
        copy.start()
        return copy

    get_state = fetch(0, state_hbm, cur)
    get_map = fetch(1, map_hbm, maps.at[me_c])
    get_diag = fetch(2, diag_hbm, diag)
    get_rim = fetch(3, rim_hbm, rim)
    get_load = fetch(4, load_hbm, load)
    get_basis = fetch(5, basis_hbm, basis)
    get_ov = fetch(6, ov_hbm, ov)
    get_count = fetch(7, count_hbm, count)
    get_inv = fetch(8, inv_hbm, inv)

    for e in range(2 * ITERS + 1):
        @pl.when(me_s == 0)
        def _():
            halo[e, 0] = jnp.zeros((rows, h), BF16)

        @pl.when(me_s == n - 1)
        def _():
            halo[e, 1] = jnp.zeros((rows, h), BF16)

    get_state.wait()
    sent[0] = cur[...].astype(BF16)
    get_map.wait()
    pl.semaphore_wait(barrier, n + m - 2)

    def to_next(e):
        return pltpu.make_async_remote_copy(
            src_ref=sent.at[e, :, pl.ds(width - h, h)], dst_ref=halo.at[e, 0],
            send_sem=halo_send.at[e, 0], recv_sem=halo_recv.at[e, 0],
            device_id={"sub": lax.rem(me_s + 1, n)}, device_id_type=MESH)

    def to_prev(e):
        return pltpu.make_async_remote_copy(
            src_ref=sent.at[e, :, pl.ds(0, h)], dst_ref=halo.at[e, 1],
            send_sem=halo_send.at[e, 1], recv_sem=halo_recv.at[e, 1],
            device_id={"sub": lax.rem(me_s + n - 1, n)}, device_id_type=MESH)

    def halo_start(e):
        @pl.when(me_s < n - 1)
        def _():
            to_next(e).start()

        @pl.when(me_s > 0)
        def _():
            to_prev(e).start()

    def halo_wait(e):
        @pl.when(me_s > 0)
        def _():
            to_next(e).wait_recv()

        @pl.when(me_s < n - 1)
        def _():
            to_prev(e).wait_recv()

    def halo_done(e):
        @pl.when(me_s < n - 1)
        def _():
            to_next(e).wait_send()

        @pl.when(me_s > 0)
        def _():
            to_prev(e).wait_send()

    relayed = m >= 4 and nc % (16 * PIECES) == 0
    pieces = PIECES if relayed else 1
    tall = nc // pieces
    upper = (2 * me_c) // m

    def map_copy(peer, slot, piece):
        return pltpu.make_async_remote_copy(
            src_ref=maps.at[slot, pl.ds(piece * tall, tall), :],
            dst_ref=maps.at[slot, pl.ds(piece * tall, tall), :],
            send_sem=map_send.at[peer, piece], recv_sem=map_recv.at[slot, piece],
            device_id={"col": peer}, device_id_type=MESH)

    def relay_copy(peer, slot, piece):
        return pltpu.make_async_remote_copy(
            src_ref=maps.at[slot, pl.ds(piece * tall, tall), :],
            dst_ref=maps.at[slot, pl.ds(piece * tall, tall), :],
            send_sem=relay_send.at[piece], recv_sem=map_recv.at[slot, piece],
            device_id={"col": peer}, device_id_type=MESH)

    def own_maps(act):
        for gap in range(m - 1 - relayed, 0, -1):
            for piece in range(pieces):
                @pl.when(me_c >= gap)
                def _():
                    act(map_copy(me_c - gap, me_c, piece))

                @pl.when(me_c + gap < m)
                def _():
                    act(map_copy(me_c + gap, me_c, piece))

    def relay(piece):
        if relayed:
            @pl.when(me_c == 1)
            def _():
                map_copy(1, m - 1, piece).wait_recv()
                relay_copy(0, m - 1, piece).start()

            @pl.when(me_c == m - 2)
            def _():
                map_copy(m - 2, 0, piece).wait_recv()
                relay_copy(m - 1, 0, piece).start()

    def relay_done():
        if relayed:
            for piece in range(pieces):
                @pl.when(me_c == 1)
                def _():
                    relay_copy(0, m - 1, piece).wait_send()

                @pl.when(me_c == m - 2)
                def _():
                    relay_copy(m - 1, 0, piece).wait_send()

    def part_copy(it, peer, slot):
        return pltpu.make_async_remote_copy(
            src_ref=part_out.at[it, peer], dst_ref=part_in.at[it, slot],
            send_sem=part_send.at[it, peer], recv_sem=part_recv.at[it, slot],
            device_id={"sub": peer}, device_id_type=MESH)

    halo_start(0)
    own_maps(lambda copy: copy.start())
    get_diag.wait()

    def stand_basis():
        block = 256
        for at in range(0, width, block):
            upright[at : at + block, :] = dot_nt(diagonal(block), basis[:, at : at + block]).astype(BF16)

    def applied(e, first):
        acc = dot(sent[e], diag[...])
        if first:
            get_basis.wait()
            stand_basis()
            get_rim.wait()
        halo_wait(e)
        return acc + dot(halo[e, 0], rim[:h]) + dot(halo[e, 1], rim[h:])

    def residual(e, first):
        acc = applied(e, first)
        if first:
            get_load.wait()
        v = cur[...]
        return load[...] - acc - cubic_coef * v * v * v

    def turn(j):
        flipped = dot_nt(diagonal(n * per), maps[j])
        if per % 16 == 0:
            for s in range(n):
                zmap[s, pl.ds(pl.multiple_of(j * per, 16), per), :] = flipped[s * per : (s + 1) * per].astype(BF16)
        else:
            turned[j] = flipped

    def turn_maps():
        for i in range(m):
            j = upper * (m - 1 - i) + (1 - upper) * i
            early = (me_c == 1) & (j == m - 1) | (me_c == m - 2) & (j == 0) if relayed else me_c < 0

            @pl.when((j != me_c) & jnp.logical_not(early))
            def _():
                for piece in range(pieces):
                    map_copy(me_c, j, piece).wait_recv()

            turn(j)
        if per % 16:
            for s in range(n):
                zmap[s] = jnp.concatenate(
                    [turned[a, s * per : (s + 1) * per, :] for a in range(m)], axis=0
                ).astype(BF16)

    def partials(it, coefficients):
        for s in range(n):
            part_out[it, s] = pack(dot_nt(coefficients, zmap[s])).astype(BF16)
        for k in range(1, n):
            part_copy(it, lax.rem(me_s + k, n), me_s).start()
        part_in[it, me_s] = part_out[it, me_s]

    def permuted_inverse():
        used = ov[...]
        slot = lax.broadcasted_iota(jnp.int32, used.shape, 1)
        used = jnp.where(slot < count[0], used, -1)
        chunk = 2 * h // 4
        for i in range(4):
            place = lax.broadcasted_iota(jnp.int32, (chunk, slots), 0) + i * chunk
            pick = (place == used).astype(F32).astype(BF16)
            invp[i * chunk : (i + 1) * chunk, :] = dot(pick, inv[half:, :]).astype(BF16)
            if i == 1 and pieces > 1:
                relay(1)

    for it in range(ITERS):
        first = it == 0
        rb = residual(2 * it, first).astype(BF16)
        e = 2 * it + 1
        sent[e] = rb
        halo_start(e)
        coefficients = dot(rb, upright[...]).astype(BF16)
        if not first:
            partials(it, coefficients)
        if first:
            relay(0)
            get_inv.wait()
            get_ov.wait()
            get_count.wait()
            permuted_inverse()
        fine = dot(rb, inv[:half, :])
        halo_wait(e)
        fine = fine + dot(halo[e, 0], invp[:h, :]) + dot(halo[e, 1], invp[h:, :])
        if first:
            for piece in range(2, pieces):
                relay(piece)
            turn_maps()
            partials(it, coefficients)
        for k in range(1, n):
            part_copy(it, me_s, lax.rem(me_s + k, n)).wait_recv()
        total = part_in[it, 0].astype(F32)
        for s in range(1, n):
            total = total + part_in[it, s].astype(F32)
        lift = dot(unpack(total, rows, nc).astype(BF16), basis[...])
        change = fine + lift
        v = cur[...] + change
        if it == ITERS - 1:
            before_ref[...] = cur[...]
            change_ref[...] = change
        else:
            cur[...] = v
        sent[e + 1] = v.astype(BF16)
        halo_start(e + 1)

    applied_ref[...] = applied(2 * ITERS, False)

    for e in range(2 * ITERS + 1):
        halo_done(e)
    own_maps(lambda copy: copy.wait_send())
    relay_done()
    for it in range(ITERS):
        for k in range(1, n):
            part_copy(it, lax.rem(me_s + k, n), me_s).wait_send()


def body(n, m, state_init, load_cols, stiff_diag, stiff_rim, inverse, ov_rows, ov_count, coarse_basis, coarse_map):
    rows, width = state_init.shape
    h = stiff_rim.shape[0] // 2
    basis_t = coarse_basis.T
    nc = basis_t.shape[0]
    trades = 2 * ITERS + 1
    hbm = pl.BlockSpec(memory_space=pltpu.HBM)
    vmem = pl.BlockSpec(memory_space=pltpu.VMEM)
    dma = pltpu.SemaphoreType.DMA
    out = jax.ShapeDtypeStruct((rows, width), F32)
    before, change, product = pl.pallas_call(
        functools.partial(kernel, n, m),
        out_shape=(out, out, out),
        in_specs=[hbm] * 9,
        out_specs=(vmem, vmem, vmem),
        scratch_shapes=[
            pltpu.VMEM((rows, width), F32),
            pltpu.VMEM((rows, width), F32),
            pltpu.VMEM(stiff_diag.shape, BF16),
            pltpu.VMEM(stiff_rim.shape, BF16),
            pltpu.VMEM(inverse.shape, BF16),
            pltpu.VMEM(ov_rows.shape, jnp.int32),
            pltpu.SMEM((1,), jnp.int32),
            pltpu.VMEM(basis_t.shape, BF16),
            pltpu.VMEM(coarse_basis.shape, BF16),
            pltpu.VMEM((m,) + coarse_map.shape, BF16),
            pltpu.VMEM((2 * h, width), BF16),
            pltpu.VMEM((m, coarse_map.shape[1], nc), F32),
            pltpu.VMEM((n, nc, nc), BF16),
            pltpu.VMEM((trades, rows, width), BF16),
            pltpu.VMEM((trades, 2, rows, h), BF16),
            pltpu.VMEM((ITERS, n) + packed_shape(rows, nc), BF16),
            pltpu.VMEM((ITERS, n) + packed_shape(rows, nc), BF16),
            dma((9,)),
            dma((trades, 2)),
            dma((trades, 2)),
            dma((m, PIECES)),
            dma((m, PIECES)),
            dma((PIECES,)),
            dma((ITERS, n)),
            dma((ITERS, n)),
        ],
        compiler_params=pltpu.CompilerParams(collective_id=0, has_side_effects=True),
        name="schwarz",
    )(state_init, load_cols, stiff_diag, stiff_rim, inverse, ov_rows, ov_count, basis_t, coarse_map)
    current = before + change
    return current, load_cols - product - cubic_coef * current * current * current


def solution(mesh):
    in_specs = (
        P("col", "sub"),
        P("col", "sub"),
        P(None, "sub"),
        P(None, "sub"),
        P(None, "sub"),
        P("sub", None),
        P("sub"),
        P("sub", None),
        P("sub", "col"),
    )
    out_specs = (P("col", "sub"), P("col", "sub"))
    step = functools.partial(body, mesh.shape["sub"], mesh.shape["col"])
    return jax.shard_map(step, mesh=mesh, in_specs=in_specs, out_specs=out_specs, check_vma=False)
```
